32 devices in a mesh: section: 4 (over y, core), tp: 8 (over z, x).
Axes of the slice: x: 2, y: 2, z: 4, core: 2. Of those that a mesh axis runs over, the one named last changes fastest.
Arguments:
- section_inputs: bfloat16 [4, 2, 64, 8192], P('section', None, 'tp'), may hold values from -6 to 6
- norm_gain: bfloat16 [4, 8192], P('section'), may hold values from 0.5 to 1.5
- w_query: bfloat16 [4, 8192, 4096], P('section', None, 'tp'), may hold values from -0.0625 to 0.0625
- key_projection: bfloat16 [4, 8192, 512], P('section', 'tp'), may hold values from -0.0625 to 0.0625
- value_projection: bfloat16 [4, 8192, 512], P('section', 'tp'), may hold values from -0.0625 to 0.0625
- w_out: bfloat16 [4, 4096, 8192], P('section', 'tp'), may hold values from -0.09375 to 0.09375
- token_dir: bfloat16 [2, 64, 8192], P(None, 'tp'), may hold values from -6 to 6
- tok_logratio: float32 [2, 64], P(None, 'tp'), may hold values from -4 to 4
- segment_ids: int32 [2, 64], replicated, may hold values from 0 to 7, as said below
- pair_of_slot: int32 [2, 4], replicated, may hold values from 0 to 7, as said below
- pair_counts: int32 [8, 2], replicated, may hold values from 1 to 24, as said below
Outputs:
- input_grads: bfloat16 [4, 2, 64, 8192], P('section', None, 'tp')
- grad_w_query: bfloat16 [4, 8192, 4096], P('section', None, 'tp')
- grad_w_key: bfloat16 [4, 8192, 512], P('section', 'tp')
- grad_w_value: bfloat16 [4, 8192, 512], P('section', 'tp')
- grad_w_out: bfloat16 [4, 4096, 8192], P('section', 'tp')
- grad_norm_gain: float32 [4, 8192], P('section')
The draws below stay inside these ranges and needn't reach their ends.
Inputs may be any that keep to these rules, and one draw needn't show every extreme that they name: `segment_ids`: in each micro-batch the segment ids do not fall along the tokens and take every value of 0 to 7; segment 2 j is the chosen and 2 j + 1 the rejected sequence of slot j; each sequence has 1 to 24 tokens and one of each micro-batch has exactly 24. `pair_of_slot`: every pair stands in exactly one slot. pair_counts[p] holds the token counts of the chosen and the rejected sequence of pair p as they stand in segment_ids.
All inputs are finite; a program needn't handle non-finite values.
Results may differ from the reference program's by a relative error of at most 0.038.
Values may be sent and summed in bfloat16 or wider, within the bound.
A program may use at most 192 MiB of HBM per device.

```python
import math
import jax
import jax.numpy as jnp
from jax import lax

MODEL_WIDTH = 8192
HEAD_WIDTH = 128
QUERY_HEAD_COUNT = 32
KEY_VALUE_HEADS = 4
MICRO = 2
SLOTS = 4
TOK_MB = 64
RELAY_SECTIONS = 4
PAIRS = 8
LONGEST = 24
N_TP = 8


def pack_layout(key):
    length_rows = []
    for batch in range(MICRO):
        branch_key = jax.random.fold_in(key, 101 + batch)
        unit_key, place_key = jax.random.split(branch_key)
        others = 2 * SLOTS - 1
        spare = LONGEST - 1
        handed = TOK_MB - LONGEST - others
        chosen_units = jax.random.permutation(unit_key, others * spare)[:handed]
        owners = chosen_units // spare
        counts = jnp.sum((owners[:, None] == jnp.arange(others, dtype=jnp.int32)[None, :]).astype(jnp.int32), 0)
        shorter = 1 + counts
        slot_place = jax.random.randint(place_key, (), 0, 2 * SLOTS)
        position = jnp.arange(2 * SLOTS, dtype=jnp.int32)
        before = jnp.take(shorter, jnp.clip(position, 0, others - 1))
        after = jnp.take(shorter, jnp.clip(position - 1, 0, others - 1))
        length_rows.append(jnp.where(position < slot_place, before, jnp.where(position == slot_place, LONGEST, after)))
    lengths = jnp.stack(length_rows).astype(jnp.int32)
    ordering = jax.random.permutation(jax.random.fold_in(key, 7), PAIRS).astype(jnp.int32)
    return (lengths, ordering)


def draw_segment_ids(key, part):
    lengths, ordering = pack_layout(key)
    ends = jnp.cumsum(lengths, 1)
    position = jnp.arange(TOK_MB, dtype=jnp.int32)
    return jnp.sum((position[None, :, None] >= ends[:, None, :-1]).astype(jnp.int32), -1).astype(jnp.int32)


def draw_pair_of_slot(key, part):
    lengths, ordering = pack_layout(key)
    return ordering.reshape(MICRO, SLOTS)


def draw_pair_counts(key, part):
    lengths, ordering = pack_layout(key)
    return jnp.zeros((PAIRS, 2), jnp.int32).at[ordering].set(lengths.reshape(PAIRS, 2))


def level_of(own_key, dims, cuts, low, largest):
    level, own = 1.0, jax.random.fold_in(own_key, 6)
    for axis_at, blocks in cuts:
        heights = jnp.exp(jax.random.uniform(jax.random.fold_in(own, axis_at), (blocks,), jnp.float32, low / len(cuts), largest / len(cuts)))
        level = level * jnp.repeat(heights, dims[axis_at] // blocks).reshape([-1 if axis == axis_at else 1 for axis in range(len(dims))])
    return level


def normal_values(rng, shape, deviation, reach, pieces=(), kind=jnp.bfloat16):
    drawn = deviation * jax.random.normal(rng, shape, jnp.float32)
    if pieces:
        drawn = drawn * level_of(rng, shape, pieces, -0.22, 0.18)
    return jnp.clip(drawn, -reach, reach).astype(kind)


def setup_inputs(seed: int = 0) -> dict:
    key_list = jax.random.split(jax.random.key(seed), 12)
    section_inputs = normal_values(key_list[0], (RELAY_SECTIONS, MICRO, TOK_MB, MODEL_WIDTH), 1.0, 6.0, ((0, 4), (2, 8)))
    norm_gain = jnp.clip(1.0 + 0.1 * jax.random.normal(key_list[1], (RELAY_SECTIONS, MODEL_WIDTH), jnp.float32), 0.5, 1.5).astype(jnp.bfloat16)
    w_query = normal_values(key_list[2], (RELAY_SECTIONS, MODEL_WIDTH, QUERY_HEAD_COUNT * HEAD_WIDTH), MODEL_WIDTH ** -0.5, 0.0625, ((0, 4), (2, 8)))
    key_projection = normal_values(key_list[3], (RELAY_SECTIONS, MODEL_WIDTH, KEY_VALUE_HEADS * HEAD_WIDTH), MODEL_WIDTH ** -0.5, 0.0625, ((0, 4), (1, 8)))
    value_projection = normal_values(key_list[4], (RELAY_SECTIONS, MODEL_WIDTH, KEY_VALUE_HEADS * HEAD_WIDTH), MODEL_WIDTH ** -0.5, 0.0625, ((0, 4), (1, 8)))
    w_out = normal_values(key_list[5], (RELAY_SECTIONS, QUERY_HEAD_COUNT * HEAD_WIDTH, MODEL_WIDTH), (QUERY_HEAD_COUNT * HEAD_WIDTH) ** -0.5, 0.09375, ((0, 4), (1, 8)))
    token_dir = normal_values(key_list[6], (MICRO, TOK_MB, MODEL_WIDTH), 1.0, 6.0, ((1, 8),))
    tok_logratio = normal_values(key_list[7], (MICRO, TOK_MB), 0.5, 4.0, ((1, 8),), jnp.float32)
    segment_ids = draw_segment_ids(jax.random.fold_in(key_list[11], 71), 0)
    pair_of_slot = draw_pair_of_slot(jax.random.fold_in(key_list[11], 71), 0)
    pair_counts = draw_pair_counts(jax.random.fold_in(key_list[11], 71), 0)
    return dict(section_inputs=section_inputs, norm_gain=norm_gain, w_query=w_query, key_projection=key_projection, value_projection=value_projection, w_out=w_out, token_dir=token_dir, tok_logratio=tok_logratio, segment_ids=segment_ids, pair_of_slot=pair_of_slot, pair_counts=pair_counts)


norm_epsilon = 1e-05
pair_beta = 4.0
masked_score = -1e+30

def rounded_down(array):
    return lax.optimization_barrier(array.astype(jnp.bfloat16)).astype(jnp.float32)

def pair_weights(seq_sums, pair_of_slot, pair_counts):
    table = (pair_of_slot[:, :, None] == jnp.arange(pair_counts.shape[0], dtype=jnp.int32)[None, None, :]).astype(jnp.float32)
    counts = jnp.einsum('msp,pc->msc', table, pair_counts.astype(jnp.float32))
    margin = pair_beta * (seq_sums[:, 0::2] / counts[:, :, 0] - seq_sums[:, 1::2] / counts[:, :, 1])
    weight = pair_beta * jax.nn.sigmoid(-margin)
    stacked = jnp.stack([-weight / counts[:, :, 0], weight / counts[:, :, 1]], -1)
    return stacked.reshape(seq_sums.shape)

def layer_backward(saved, gain_row, query_weight, key_weight, value_weight, out_weight, upstream, allowed):
    query_group = QUERY_HEAD_COUNT // KEY_VALUE_HEADS
    scale = 1.0 / math.sqrt(HEAD_WIDTH)
    batch_groups = saved.shape[0]
    token_total = saved.shape[1]
    inputs = saved.astype(jnp.float32)
    inverse_rms = lax.rsqrt(lax.optimization_barrier(jnp.mean(inputs * inputs, -1, keepdims=True)) + norm_epsilon)
    unit_rows = inputs * inverse_rms
    gain_values = gain_row.astype(jnp.float32)
    normed_wide = rounded_down(unit_rows * gain_values)
    queries = rounded_down(jnp.einsum('mtd,dc->mtc', normed_wide, query_weight.astype(jnp.float32)))
    key_tensor = rounded_down(jnp.einsum('mtd,dc->mtc', normed_wide, key_weight.astype(jnp.float32)))
    value_tensor = rounded_down(jnp.einsum('mtd,dc->mtc', normed_wide, value_weight.astype(jnp.float32)))
    query_heads = queries.reshape(batch_groups, token_total, QUERY_HEAD_COUNT, HEAD_WIDTH)
    heads_of_key = jnp.repeat(key_tensor.reshape(batch_groups, token_total, KEY_VALUE_HEADS, HEAD_WIDTH), query_group, axis=2)
    heads_of_value = jnp.repeat(value_tensor.reshape(batch_groups, token_total, KEY_VALUE_HEADS, HEAD_WIDTH), query_group, axis=2)
    scores = jnp.einsum('mthc,muhc->mhtu', query_heads, heads_of_key) * scale
    scores = jnp.where(allowed[:, None], scores, masked_score)
    softmax_rows = jnp.exp(scores)
    softmax_rows = softmax_rows / lax.optimization_barrier(jnp.sum(softmax_rows, -1, keepdims=True))
    soft_low = rounded_down(softmax_rows)
    attended = rounded_down(jnp.einsum('mhtu,muhc->mthc', soft_low, heads_of_value)).reshape(batch_groups, token_total, QUERY_HEAD_COUNT * HEAD_WIDTH)
    upstream_wide = upstream.astype(jnp.float32)
    grad_attended = rounded_down(jnp.einsum('mtd,cd->mtc', upstream_wide, out_weight.astype(jnp.float32)))
    grad_heads = grad_attended.reshape(batch_groups, token_total, QUERY_HEAD_COUNT, HEAD_WIDTH)
    grad_probs = jnp.einsum('mthc,muhc->mhtu', grad_heads, heads_of_value)
    grad_scores = softmax_rows * (grad_probs - lax.optimization_barrier(jnp.sum(softmax_rows * grad_probs, -1, keepdims=True)))
    scores_low = rounded_down(grad_scores * scale)
    grad_queries = rounded_down(jnp.einsum('mhtu,muhc->mthc', scores_low, heads_of_key)).reshape(batch_groups, token_total, QUERY_HEAD_COUNT * HEAD_WIDTH)
    key_summands = jnp.einsum('mhtu,mthc->muhc', scores_low, query_heads)
    key_gradient = rounded_down(key_summands.reshape(batch_groups, token_total, KEY_VALUE_HEADS, query_group, HEAD_WIDTH).sum(3).reshape(batch_groups, token_total, KEY_VALUE_HEADS * HEAD_WIDTH))
    value_summands = jnp.einsum('mhtu,mthc->muhc', soft_low, grad_heads)
    value_gradient = rounded_down(value_summands.reshape(batch_groups, token_total, KEY_VALUE_HEADS, query_group, HEAD_WIDTH).sum(3).reshape(batch_groups, token_total, KEY_VALUE_HEADS * HEAD_WIDTH))
    per_device = QUERY_HEAD_COUNT * HEAD_WIDTH // N_TP
    query_parts = grad_queries.reshape(batch_groups, token_total, N_TP, per_device).transpose(2, 0, 1, 3)
    weight_parts = query_weight.astype(jnp.float32).reshape(MODEL_WIDTH, N_TP, per_device).transpose(1, 0, 2)

    def add_part(total, members):
        part, weight_part = members
        return (total + rounded_down(jnp.einsum('mtc,dc->mtd', part, weight_part)), None)
    grad_normed, unused = lax.scan(add_part, jnp.zeros((batch_groups, token_total, MODEL_WIDTH), jnp.float32), (query_parts, weight_parts))
    key_path = jnp.einsum('mtk,dk->mtd', key_gradient, key_weight.astype(jnp.float32)) + jnp.einsum('mtk,dk->mtd', value_gradient, value_weight.astype(jnp.float32))
    grad_normed = grad_normed + rounded_down(key_path)
    grad_unit = grad_normed * gain_values
    grad_input = (upstream_wide + inverse_rms * (grad_unit - unit_rows * lax.optimization_barrier(jnp.mean(grad_unit * unit_rows, -1, keepdims=True)))).astype(jnp.bfloat16)
    grad_query_w = jnp.einsum('mtd,mtc->dc', normed_wide, grad_queries).astype(jnp.bfloat16)
    grad_key_w = jnp.einsum('mtd,mtc->dc', normed_wide, key_gradient).astype(jnp.bfloat16)
    grad_value_w = jnp.einsum('mtd,mtc->dc', normed_wide, value_gradient).astype(jnp.bfloat16)
    grad_out_w = jnp.einsum('mtc,mtd->cd', attended, upstream_wide).astype(jnp.bfloat16)
    grad_gain = lax.optimization_barrier(jnp.sum(grad_normed * unit_rows, (0, 1)))
    return (grad_input, grad_query_w, grad_key_w, grad_value_w, grad_out_w, grad_gain)

def reference(section_inputs, norm_gain, w_query, key_projection, value_projection, w_out, token_dir, tok_logratio, segment_ids, pair_of_slot, pair_counts):
    seq_count = 2 * SLOTS
    member = (segment_ids[:, :, None] == jnp.arange(seq_count, dtype=jnp.int32)[None, None, :]).astype(jnp.float32)
    seq_sums = jnp.einsum('mt,mts->ms', tok_logratio.astype(jnp.float32), member)
    weights = pair_weights(seq_sums, pair_of_slot, pair_counts)
    token_weight = jnp.einsum('mts,ms->mt', member, weights)
    upstream = (token_weight[:, :, None] * token_dir.astype(jnp.float32)).astype(jnp.bfloat16)
    position = jnp.arange(TOK_MB, dtype=jnp.int32)
    allowed = (segment_ids[:, :, None] == segment_ids[:, None, :]) & (position[:, None] >= position[None, :])[None]
    results = [None] * RELAY_SECTIONS
    for section in reversed(range(RELAY_SECTIONS)):
        results[section] = layer_backward(section_inputs[section], norm_gain[section], w_query[section], key_projection[section], value_projection[section], w_out[section], upstream, allowed)
        upstream = results[section][0]
    gathered = [jnp.stack([entry[number] for entry in results]) for number in range(6)]
    return (gathered[0], gathered[1], gathered[2], gathered[3], gathered[4], gathered[5])
```

```python
import functools
import math

import jax
import jax.numpy as jnp
from jax import lax
from jax.experimental import pallas as pl
from jax.experimental.pallas import tpu as pltpu
from jax.sharding import PartitionSpec as P

HEAD_WIDTH = 128
QUERY_HEAD_COUNT = 32
SLOTS = 4


norm_epsilon = 1e-05
pair_beta = 4.0
masked_score = -1e30


def pair_weights(seq_sums, pair_of_slot, pair_counts):
    table = (
        pair_of_slot[:, :, None] == jnp.arange(pair_counts.shape[0], dtype=jnp.int32)[None, None, :]
    ).astype(jnp.float32)
    counts = jnp.einsum("msp,pc->msc", table, pair_counts.astype(jnp.float32))
    margin = pair_beta * (seq_sums[:, 0::2] / counts[:, :, 0] - seq_sums[:, 1::2] / counts[:, :, 1])
    weight = pair_beta * jax.nn.sigmoid(-margin)
    stacked = jnp.stack([-weight / counts[:, :, 0], weight / counts[:, :, 1]], -1)
    return stacked.reshape(seq_sums.shape)


def contract_last(left, right):
    return lax.dot_general(
        left, right, (((1,), (1,)), ((), ())), preferred_element_type=jnp.float32
    )


MESH = pl.DeviceIdType.MESH
VMEM_LIMIT = 48 * 1024 * 1024


def exchange_kernel(kinds, tp_count, group, section_count, *refs):
    count = len(kinds)
    ins, outs = refs[:count], refs[count : 2 * count]
    send_sem, recv_sem = refs[2 * count :]
    sec = lax.axis_index("section")
    me = lax.axis_index("tp")
    barrier = pltpu.get_barrier_semaphore()
    for d in range(1, tp_count):
        pl.semaphore_signal(
            barrier, inc=1, device_id=(sec, lax.rem(me + d, tp_count)), device_id_type=MESH
        )
    pl.semaphore_wait(barrier, tp_count - 1)

    def copies(a):
        made = []
        for d in range(1, tp_count):
            peer = lax.rem(me + d, tp_count)
            source = ins[a].at[peer // group] if kinds[a] == "pick" else ins[a]
            made.append(
                pltpu.make_async_remote_copy(
                    src_ref=source,
                    dst_ref=outs[a].at[me],
                    send_sem=send_sem.at[a, d],
                    recv_sem=recv_sem.at[a, d],
                    device_id=(sec, peer),
                    device_id_type=MESH,
                )
            )
        return made

    def send(a):
        for copy in copies(a):
            copy.start()
        outs[a][me] = ins[a][me // group] if kinds[a] == "pick" else ins[a][...]

    def receive(a):
        for copy in copies(a):
            copy.wait()

    for step in (send, receive):
        for a in range(count):
            if kinds[a] == "last":
                pl.when(sec == section_count - 1)(functools.partial(step, a))
            else:
                step(a)


def exchange(arrays, kinds, group, identity):
    tp_count = lax.axis_size("tp")
    shapes = [
        jax.ShapeDtypeStruct(
            (tp_count,) + (a.shape[1:] if kind == "pick" else a.shape), a.dtype
        )
        for a, kind in zip(arrays, kinds)
    ]
    vmem = pl.BlockSpec(memory_space=pltpu.VMEM)
    return pl.pallas_call(
        functools.partial(exchange_kernel, kinds, tp_count, group, lax.axis_size("section")),
        out_shape=shapes,
        in_specs=[vmem] * len(arrays),
        out_specs=[vmem] * len(arrays),
        scratch_shapes=[
            pltpu.SemaphoreType.DMA((len(arrays), tp_count)),
            pltpu.SemaphoreType.DMA((len(arrays), tp_count)),
        ],
        compiler_params=pltpu.CompilerParams(
            collective_id=identity, has_side_effects=True, vmem_limit_bytes=VMEM_LIMIT
        ),
        name=f"exchange_{identity}",
    )(*arrays)


def relay_kernel(
    turn,
    batch_groups,
    section_count,
    tp_count,
    part_ref,
    dkv_ref,
    g_ref,
    saved_ref,
    gain_ref,
    kw_ref,
    vw_ref,
    gin_ref,
    gnext_ref,
    dkv_full_ref,
    gain_out_ref,
    part_recv,
    dkv_recv,
    ks_send,
    ks_recv,
    grad_unit,
    unit,
    p_send,
    p_recv,
    d_send,
    d_recv,
    k_send,
    k_recv,
    g_send,
    g_recv,
):
    sec = lax.axis_index("section")
    me = lax.axis_index("tp")
    rows, width = gin_ref.shape
    slice_width = kw_ref.shape[0]
    key_width = kw_ref.shape[1]
    key_count = key_width // HEAD_WIDTH
    sharers = tp_count // key_count
    first = section_count - 1 - turn
    active = (sec >= first) & (sec < first + batch_groups)
    fed = (sec + 1 >= first) & (sec + 1 < first + batch_groups) & (sec < section_count - 1)
    feeds = active & (sec > 0)
    barrier = pltpu.get_barrier_semaphore()

    def peer(d):
        return lax.rem(me + d, tp_count)

    @pl.when(active)
    def _():
        for d in range(1, tp_count):
            pl.semaphore_signal(barrier, inc=1, device_id=(sec, peer(d)), device_id_type=MESH)

    @pl.when(fed)
    def _():
        for d in range(tp_count):
            pl.semaphore_signal(barrier, inc=1, device_id=(sec + 1, peer(d)), device_id_type=MESH)

    def remote(source, target, sends, receives, d, section):
        return pltpu.make_async_remote_copy(
            src_ref=source,
            dst_ref=target,
            send_sem=sends.at[d],
            recv_sem=receives.at[d],
            device_id=(section, peer(d)),
            device_id_type=MESH,
        )

    def part_copy(d):
        return remote(part_ref.at[peer(d)], part_recv.at[me], p_send, p_recv, d, sec)

    def dkv_copy(d):
        return remote(dkv_ref, dkv_recv.at[me], d_send, d_recv, d, sec)

    def ks_copy(d):
        return remote(ks_send.at[peer(d)], ks_recv.at[me], k_send, k_recv, d, sec)

    @pl.when(feeds)
    def _():
        pl.semaphore_wait(barrier, 2 * tp_count - 1)

    @pl.when(active & (sec == 0))
    def _():
        pl.semaphore_wait(barrier, tp_count - 1)

    @pl.when(active)
    def _():
        for d in range(1, tp_count):
            dkv_copy(d).start()
        for d in range(1, tp_count):
            part_copy(d).start()
        dkv_recv[me] = dkv_ref[...]
        part_recv[me] = part_ref[me]
        x = saved_ref[...].astype(jnp.float32)
        inverse = lax.rsqrt(jnp.mean(x * x, -1, keepdims=True) + norm_epsilon)
        unit[...] = x * inverse
        for d in range(1, tp_count):
            dkv_copy(d).wait()
        for kind in range(2):
            for k in range(key_count):
                total = dkv_recv[k * sharers, kind].astype(jnp.float32)
                for other in range(1, sharers):
                    total = total + dkv_recv[k * sharers + other, kind].astype(jnp.float32)
                dkv_full_ref[kind, :, k * HEAD_WIDTH : (k + 1) * HEAD_WIDTH] = total.astype(
                    jnp.bfloat16
                )
        key_slice = contract_last(dkv_full_ref[0], kw_ref[...]) + contract_last(
            dkv_full_ref[1], vw_ref[...]
        )
        for j in range(tp_count):
            ks_send[j] = key_slice[j * rows : (j + 1) * rows].astype(jnp.bfloat16)
        for d in range(1, tp_count):
            ks_copy(d).start()
        ks_recv[me] = ks_send[me]
        for d in range(1, tp_count):
            part_copy(d).wait()
        for d in range(1, tp_count):
            ks_copy(d).wait()
        dots = jnp.zeros((rows, 1), jnp.float32)
        for i in range(tp_count):
            cols = slice(i * slice_width, (i + 1) * slice_width)
            normed_grad = ks_recv[i].astype(jnp.float32) + jnp.sum(
                part_recv[:, :, cols].astype(jnp.float32), 0
            )
            unit_part = unit[:, cols]
            gain_out_ref[:, cols] = jnp.sum(normed_grad * unit_part, 0, keepdims=True)
            scaled = normed_grad * gain_ref[:, cols].astype(jnp.float32)
            grad_unit[:, cols] = scaled
            dots = dots + jnp.sum(scaled * unit_part, -1, keepdims=True)
        dots = dots / width
        for i in range(tp_count):
            cols = slice(i * slice_width, (i + 1) * slice_width)
            gin_ref[:, cols] = (
                g_ref[me, :, cols].astype(jnp.float32)
                + inverse * (grad_unit[:, cols] - unit[:, cols] * dots)
            ).astype(jnp.bfloat16)

    @pl.when(feeds)
    def _():
        for d in range(tp_count):
            remote(gin_ref, gnext_ref.at[me], g_send, g_recv, d, sec - 1).start()
        for d in range(tp_count):
            remote(gin_ref, gnext_ref.at[me], g_send, g_recv, d, sec - 1).wait_send()

    @pl.when(fed)
    def _():
        for d in range(tp_count):
            remote(gin_ref, gnext_ref.at[me], g_send, g_recv, d, sec).wait_recv()


def relay(turn, batch_groups, identity, part, dkv, g, saved, gain, kw, vw):
    tp_count, rows, width = part.shape
    tokens = dkv.shape[1]
    slice_width, key_width = kw.shape
    vmem = pl.BlockSpec(memory_space=pltpu.VMEM)
    dma = pltpu.SemaphoreType.DMA((tp_count,))
    low = jnp.bfloat16
    return pl.pallas_call(
        functools.partial(relay_kernel, turn, batch_groups, lax.axis_size("section"), tp_count),
        out_shape=[
            jax.ShapeDtypeStruct((rows, width), low),
            jax.ShapeDtypeStruct((tp_count, rows, width), low),
            jax.ShapeDtypeStruct((2, tokens, key_width), low),
            jax.ShapeDtypeStruct((1, width), jnp.float32),
        ],
        in_specs=[vmem] * 7,
        out_specs=[vmem] * 4,
        scratch_shapes=[
            pltpu.VMEM((tp_count, rows, width), low),
            pltpu.VMEM((tp_count, 2, tokens, HEAD_WIDTH), low),
            pltpu.VMEM((tp_count, rows, slice_width), low),
            pltpu.VMEM((tp_count, rows, slice_width), low),
            pltpu.VMEM((rows, width), jnp.float32),
            pltpu.VMEM((rows, width), jnp.float32),
        ]
        + [dma] * 8,
        compiler_params=pltpu.CompilerParams(
            collective_id=identity, has_side_effects=True, vmem_limit_bytes=VMEM_LIMIT
        ),
        name=f"relay_{turn}",
    )(*lax.optimization_barrier((part, dkv, g, saved, gain, kw, vw)))


def body(
    section_inputs,
    norm_gain,
    w_query,
    key_projection,
    value_projection,
    w_out,
    token_dir,
    tok_logratio,
    segment_ids,
    pair_of_slot,
    pair_counts,
):
    low, wide = jnp.bfloat16, jnp.float32
    section_count = lax.axis_size("section")
    tp_count = lax.axis_size("tp")
    section_index = lax.axis_index("section")
    tp_index = lax.axis_index("tp")
    saved = section_inputs[0]
    batch_groups, rows, width = saved.shape
    token_total = rows * tp_count
    every = batch_groups * token_total
    gain_values = norm_gain[0].astype(wide)
    query_weight = w_query[0]
    key_weight = key_projection[0]
    value_weight = value_projection[0]
    out_weight = w_out[0]
    head_cols = query_weight.shape[1]
    local_heads = head_cols // HEAD_WIDTH
    slice_width, key_width = key_weight.shape
    key_count = key_width // HEAD_WIDTH
    sharers = tp_count // key_count
    seq_count = 2 * SLOTS
    scale = 1.0 / math.sqrt(HEAD_WIDTH)

    ratio_rows = jnp.broadcast_to(tok_logratio.reshape(-1, 1), (batch_groups * rows, 128))
    saved_all, ratio_all, dir_all = exchange(
        (saved, ratio_rows, token_dir), ("all", "all", "last"), 1, 0
    )
    whole = saved_all.transpose(1, 0, 2, 3).reshape(every, width)
    ratios = (
        ratio_all[:, :, 0]
        .reshape(tp_count, batch_groups, rows)
        .transpose(1, 0, 2)
        .reshape(batch_groups, token_total)
    )
    whole_wide = whole.astype(wide)
    whole_inverse = lax.rsqrt(jnp.mean(whole_wide * whole_wide, -1, keepdims=True) + norm_epsilon)
    normed = (whole_wide * whole_inverse * gain_values).astype(low)
    normed_cols = lax.dynamic_slice_in_dim(normed, tp_index * slice_width, slice_width, 1)
    kv_part = jnp.stack(
        [
            jnp.dot(normed_cols, weight, preferred_element_type=wide)
            .astype(low)
            .reshape(every, key_count, HEAD_WIDTH)
            .transpose(1, 0, 2)
            for weight in (key_weight, value_weight)
        ],
        1,
    )
    (kv_all,) = exchange((kv_part,), ("pick",), sharers, 1)
    kv = jnp.sum(kv_all.astype(wide), 0).astype(low)
    keys = kv[0].reshape(batch_groups, token_total, HEAD_WIDTH)
    values = kv[1].reshape(batch_groups, token_total, HEAD_WIDTH)
    queries = jnp.dot(normed, query_weight, preferred_element_type=wide).astype(low)

    member = (
        segment_ids[:, :, None] == jnp.arange(seq_count, dtype=jnp.int32)[None, None, :]
    ).astype(wide)
    seq_sums = jnp.sum(ratios[:, :, None] * member, 1)
    weights = pair_weights(seq_sums, pair_of_slot, pair_counts)
    token_weight = jnp.sum(member * weights[:, None, :], -1)
    top = (
        token_weight.reshape(batch_groups, tp_count, rows)[:, :, :, None]
        * dir_all.transpose(1, 0, 2, 3).astype(wide)
    ).astype(low)

    query_heads = queries.reshape(batch_groups, token_total, local_heads, HEAD_WIDTH)
    position = jnp.arange(token_total, dtype=jnp.int32)
    allowed = (segment_ids[:, :, None] == segment_ids[:, None, :]) & (
        position[:, None] >= position[None, :]
    )[None]
    scores = jnp.einsum("mthc,muc->mhtu", query_heads, keys, preferred_element_type=wide) * scale
    scores = jnp.where(allowed[:, None], scores, masked_score)
    probs = jnp.exp(scores)
    probs = probs / jnp.sum(probs, -1, keepdims=True)
    probs_low = probs.astype(low)
    attended = (
        jnp.einsum("mhtu,muc->mthc", probs_low, values, preferred_element_type=wide)
        .astype(low)
        .reshape(every, head_cols)
    )
    is_last = section_index == section_count - 1
    gain_row = norm_gain[0].reshape(1, width)

    def select(array, pick):
        return lax.dynamic_index_in_dim(array, pick, 0, keepdims=False)

    boundary = jnp.zeros((tp_count, rows, width), low)
    turns = []
    for turn in range(section_count + batch_groups - 1):
        pick = jnp.clip(turn - (section_count - 1 - section_index), 0, batch_groups - 1)
        incoming = jnp.where(is_last, top[min(turn, batch_groups - 1)], boundary)
        upstream = incoming.reshape(token_total, width)
        grad_heads = (
            contract_last(upstream, out_weight)
            .astype(low)
            .reshape(token_total, local_heads, HEAD_WIDTH)
        )
        query_now = select(query_heads, pick)
        key_now = select(keys, pick)
        value_now = select(values, pick)
        probs_now = select(probs, pick)
        probs_low_now = select(probs_low, pick)
        grad_probs = jnp.einsum("thc,uc->htu", grad_heads, value_now, preferred_element_type=wide)
        grad_scores = probs_now * (
            grad_probs - jnp.sum(probs_now * grad_probs, -1, keepdims=True)
        )
        scores_low = (grad_scores * scale).astype(low)
        grad_query = (
            jnp.einsum("htu,uc->thc", scores_low, key_now, preferred_element_type=wide)
            .astype(low)
            .reshape(token_total, head_cols)
        )
        dkv = jnp.stack(
            [
                jnp.einsum("htu,thc->uc", scores_low, query_now, preferred_element_type=wide),
                jnp.einsum("htu,thc->uc", probs_low_now, grad_heads, preferred_element_type=wide),
            ]
        ).astype(low)
        part = contract_last(grad_query, query_weight).astype(low)
        relayed = relay(
            turn,
            batch_groups,
            2 + turn,
            part.reshape(tp_count, rows, width),
            dkv,
            incoming,
            select(saved, pick),
            gain_row,
            key_weight,
            value_weight,
        )
        grad_rows, boundary, dkv_full, gain_part = lax.optimization_barrier(tuple(relayed))
        turns.append((grad_rows, upstream, dkv_full, gain_part, grad_query))

    begin = section_count - 1 - section_index
    grads, upstreams, dkvs, gains, grad_queries = (
        lax.dynamic_slice_in_dim(jnp.stack(values_of), begin, batch_groups, 0)
        for values_of in zip(*turns)
    )
    gain_total = jnp.sum(gains, 0).reshape(8, width // 8)
    (gain_all,) = exchange((gain_total,), ("all",), 1, 2 + len(turns))
    outer = functools.partial(
        lax.dot_general,
        dimension_numbers=(((0,), (0,)), ((), ())),
        preferred_element_type=wide,
    )
    return (
        grads[None],
        outer(normed, grad_queries.reshape(every, head_cols)).astype(low)[None],
        outer(normed_cols, dkvs[:, 0].reshape(every, key_width)).astype(low)[None],
        outer(normed_cols, dkvs[:, 1].reshape(every, key_width)).astype(low)[None],
        outer(attended, upstreams.reshape(every, width)).astype(low)[None],
        jnp.sum(gain_all, 0).reshape(1, width),
    )


def solution(mesh):
    placed = (
        P("section", None, "tp", None),
        P("section", None),
        P("section", None, "tp"),
        P("section", "tp", None),
        P("section", "tp", None),
        P("section", "tp", None),
        P(None, "tp", None),
        P(None, "tp"),
        P(),
        P(),
        P(),
    )
    return jax.shard_map(
        body,
        mesh=mesh,
        in_specs=placed,
        out_specs=(
            P("section", None, "tp", None),
            P("section", None, "tp"),
            P("section", "tp", None),
            P("section", "tp", None),
            P("section", "tp", None),
            P("section", None),
        ),
        check_vma=False,
    )
```

```python
import functools
import math

import jax
import jax.numpy as jnp
from jax import lax
from jax.experimental import pallas as pl
from jax.experimental.pallas import tpu as pltpu
from jax.sharding import PartitionSpec as P

HEAD_WIDTH = 128
QUERY_HEAD_COUNT = 32
SLOTS = 4


norm_epsilon = 1e-05
pair_beta = 4.0
masked_score = -1e30


def pair_weights(seq_sums, pair_of_slot, pair_counts):
    table = (
        pair_of_slot[:, :, None] == jnp.arange(pair_counts.shape[0], dtype=jnp.int32)[None, None, :]
    ).astype(jnp.float32)
    counts = jnp.einsum("msp,pc->msc", table, pair_counts.astype(jnp.float32))
    margin = pair_beta * (seq_sums[:, 0::2] / counts[:, :, 0] - seq_sums[:, 1::2] / counts[:, :, 1])
    weight = pair_beta * jax.nn.sigmoid(-margin)
    stacked = jnp.stack([-weight / counts[:, :, 0], weight / counts[:, :, 1]], -1)
    return stacked.reshape(seq_sums.shape)


def contract_last(left, right):
    return lax.dot_general(
        left, right, (((1,), (1,)), ((), ())), preferred_element_type=jnp.float32
    )


MESH = pl.DeviceIdType.MESH
VMEM_LIMIT = 48 * 1024 * 1024


def inner_size(tp_count):
    inner = 1
    while 2 * (2 * inner) ** 2 <= tp_count:
        inner *= 2
    return inner


def exchange_kernel(kinds, tp_count, group, section_count, *refs):
    count = len(kinds)
    ins, outs = refs[:count], refs[count : 2 * count]
    send_sem, recv_sem, first_send, first_recv = refs[2 * count :]
    sec = lax.axis_index("section")
    me = lax.axis_index("tp")
    inner = inner_size(tp_count)
    outer = tp_count // inner
    z, x = me // inner, lax.rem(me, inner)
    barrier = pltpu.get_barrier_semaphore()
    for d in range(1, tp_count):
        pl.semaphore_signal(
            barrier, inc=1, device_id=(sec, lax.rem(me + d, tp_count)), device_id_type=MESH
        )
    pl.semaphore_wait(barrier, tp_count - 1)

    def columns(index):
        head = pl.multiple_of(index // group * HEAD_WIDTH, HEAD_WIDTH)
        return pl.ds(head, HEAD_WIDTH)

    def pick_copy(a, d):
        peer = lax.rem(me + d, tp_count)
        return pltpu.make_async_remote_copy(
            src_ref=ins[a].at[:, columns(peer)],
            dst_ref=outs[a].at[me],
            send_sem=send_sem.at[a, d],
            recv_sem=recv_sem.at[a, d],
            device_id=(sec, peer),
            device_id_type=MESH,
        )

    def far_copy(a, zd):
        return pltpu.make_async_remote_copy(
            src_ref=ins[a],
            dst_ref=outs[a].at[me],
            send_sem=first_send.at[a, zd],
            recv_sem=first_recv.at[a, zd],
            device_id=(sec, lax.rem(z + zd, outer) * inner + x),
            device_id_type=MESH,
        )

    def near_copy(a, zd, xd):
        block = lax.rem(z - zd + outer, outer) * inner + x
        return pltpu.make_async_remote_copy(
            src_ref=outs[a].at[block] if zd else ins[a],
            dst_ref=outs[a].at[block],
            send_sem=send_sem.at[a, zd * inner + xd],
            recv_sem=recv_sem.at[a, zd * inner + xd],
            device_id=(sec, z * inner + lax.rem(x + xd, inner)),
            device_id_type=MESH,
        )

    def send(a):
        if kinds[a] == "pick":
            for d in range(1, tp_count):
                pick_copy(a, d).start()
            outs[a][me] = ins[a][:, columns(me)]
            return
        for zd in range(1, outer):
            far_copy(a, zd).start()
        for xd in range(1, inner):
            near_copy(a, 0, xd).start()
        outs[a][me] = ins[a][...]

    def forward(a):
        if kinds[a] == "pick":
            return
        for zd in range(1, outer):
            far_copy(a, zd).wait()
            for xd in range(1, inner):
                near_copy(a, zd, xd).start()

    def receive(a):
        if kinds[a] == "pick":
            for d in range(1, tp_count):
                pick_copy(a, d).wait()
            return
        for zd in range(outer):
            for xd in range(1, inner):
                near_copy(a, zd, xd).wait()

    for step in (send, forward, receive):
        for a in range(count):
            if kinds[a] == "last":
                pl.when(sec == section_count - 1)(functools.partial(step, a))
            else:
                step(a)


def exchange(arrays, kinds, group, identity):
    tp_count = lax.axis_size("tp")
    shapes = [
        jax.ShapeDtypeStruct(
            (tp_count,) + ((a.shape[0], HEAD_WIDTH) if kind == "pick" else a.shape), a.dtype
        )
        for a, kind in zip(arrays, kinds)
    ]
    vmem = pl.BlockSpec(memory_space=pltpu.VMEM)
    return pl.pallas_call(
        functools.partial(exchange_kernel, kinds, tp_count, group, lax.axis_size("section")),
        out_shape=shapes,
        in_specs=[vmem] * len(arrays),
        out_specs=[vmem] * len(arrays),
        scratch_shapes=[pltpu.SemaphoreType.DMA((len(arrays), tp_count)) for _ in range(4)],
        compiler_params=pltpu.CompilerParams(
            collective_id=identity, has_side_effects=True, vmem_limit_bytes=VMEM_LIMIT
        ),
        name=f"exchange_{identity}",
    )(*arrays)


def relay_kernel(
    turn,
    batch_groups,
    section_count,
    tp_count,
    part_ref,
    dkv_ref,
    g_ref,
    saved_ref,
    gain_ref,
    kw_ref,
    vw_ref,
    gin_ref,
    gnext_ref,
    dkv_full_ref,
    gain_out_ref,
    near_recv,
    far_send,
    far_recv,
    dkv_recv,
    ks_send,
    ks_recv,
    grad_unit,
    unit,
    p_send,
    p_recv,
    q_send,
    q_recv,
    d_send,
    d_recv,
    k_send,
    k_recv,
    g_send,
    g_recv,
    f_send,
    f_recv,
):
    sec = lax.axis_index("section")
    me = lax.axis_index("tp")
    rows, width = gin_ref.shape
    slice_width = kw_ref.shape[0]
    key_width = kw_ref.shape[1]
    key_count = key_width // HEAD_WIDTH
    sharers = tp_count // key_count
    first = section_count - 1 - turn
    active = (sec >= first) & (sec < first + batch_groups)
    fed = (sec + 1 >= first) & (sec + 1 < first + batch_groups) & (sec < section_count - 1)
    feeds = active & (sec > 0)
    barrier = pltpu.get_barrier_semaphore()

    def peer(d):
        return lax.rem(me + d, tp_count)

    inner = inner_size(tp_count)
    outer = tp_count // inner
    z, x = me // inner, lax.rem(me, inner)

    def far(zd):
        return lax.rem(z + zd, outer) * inner + x

    def near(xd):
        return z * inner + lax.rem(x + xd, inner)

    def greet(section, index):
        pl.semaphore_signal(barrier, inc=1, device_id=(section, index), device_id_type=MESH)

    @pl.when(active)
    def _():
        for d in range(1, tp_count):
            greet(sec, peer(d))

    @pl.when(fed & (sec < first))
    def _():
        for xd in range(1, inner):
            greet(sec, near(xd))

    @pl.when(fed)
    def _():
        for zd in range(outer):
            greet(sec + 1, far(zd))

    def remote(source, target, sends, receives, d, section, index):
        return pltpu.make_async_remote_copy(
            src_ref=source,
            dst_ref=target,
            send_sem=sends.at[d],
            recv_sem=receives.at[d],
            device_id=(section, index),
            device_id_type=MESH,
        )

    def near_part(zd, xd):
        slot = zd * inner + xd
        block = lax.rem(z + zd, outer) * inner + lax.rem(x + xd, inner)
        return remote(
            part_ref.at[block], near_recv.at[slot], p_send, p_recv, slot, sec, near(xd)
        )

    def far_part(zd):
        return remote(far_send.at[zd], far_recv.at[zd], q_send, q_recv, zd, sec, far(zd))

    def next_copy(zd, section):
        return remote(gin_ref, gnext_ref.at[me], g_send, g_recv, zd, section, far(zd))

    def next_forward(zd, xd):
        block = gnext_ref.at[lax.rem(z - zd + outer, outer) * inner + x]
        return remote(block, block, f_send, f_recv, zd * inner + xd, sec, near(xd))

    def dkv_copy(d):
        return remote(dkv_ref, dkv_recv.at[me], d_send, d_recv, d, sec, peer(d))

    def ks_copy(d):
        return remote(ks_send.at[peer(d)], ks_recv.at[me], k_send, k_recv, d, sec, peer(d))

    @pl.when(feeds)
    def _():
        pl.semaphore_wait(barrier, tp_count - 1 + outer)

    @pl.when(active & (sec == 0))
    def _():
        pl.semaphore_wait(barrier, tp_count - 1)

    @pl.when(fed & (sec < first))
    def _():
        pl.semaphore_wait(barrier, inner - 1)

    @pl.when(active)
    def _():
        for d in range(1, tp_count):
            dkv_copy(d).start()
        order = [*range(1, outer), 0]
        for zd in order:
            for xd in range(1, inner):
                near_part(zd, xd).start()
        dkv_recv[me] = dkv_ref[...]
        rows_in = saved_ref[...].astype(jnp.float32)
        inverse = lax.rsqrt(jnp.mean(rows_in * rows_in, -1, keepdims=True) + norm_epsilon)
        unit[...] = rows_in * inverse
        for d in range(1, tp_count):
            dkv_copy(d).wait()
        for kind in range(2):
            for k in range(key_count):
                total = dkv_recv[k * sharers, kind].astype(jnp.float32)
                for other in range(1, sharers):
                    total = total + dkv_recv[k * sharers + other, kind].astype(jnp.float32)
                dkv_full_ref[kind, :, k * HEAD_WIDTH : (k + 1) * HEAD_WIDTH] = total.astype(
                    jnp.bfloat16
                )
        key_slice = contract_last(dkv_full_ref[0], kw_ref[...]) + contract_last(
            dkv_full_ref[1], vw_ref[...]
        )
        for j in range(tp_count):
            ks_send[j] = key_slice[j * rows : (j + 1) * rows].astype(jnp.bfloat16)
        for d in range(1, tp_count):
            ks_copy(d).start()
        ks_recv[me] = ks_send[me]
        for zd in order:
            total = part_ref[far(zd)].astype(jnp.float32)
            for xd in range(1, inner):
                near_part(zd, xd).wait()
                total = total + near_recv[zd * inner + xd].astype(jnp.float32)
            if zd:
                far_send[zd] = total.astype(jnp.bfloat16)
                far_part(zd).start()
            else:
                far_recv[0] = total.astype(jnp.bfloat16)
        for zd in range(1, outer):
            far_part(zd).wait()
        for d in range(1, tp_count):
            ks_copy(d).wait()
        dots = jnp.zeros((rows, 1), jnp.float32)
        for i in range(tp_count):
            cols = slice(i * slice_width, (i + 1) * slice_width)
            normed_grad = ks_recv[i].astype(jnp.float32) + jnp.sum(
                far_recv[:, :, cols].astype(jnp.float32), 0
            )
            unit_part = unit[:, cols]
            gain_out_ref[:, cols] = jnp.sum(normed_grad * unit_part, 0, keepdims=True)
            scaled = normed_grad * gain_ref[:, cols].astype(jnp.float32)
            grad_unit[:, cols] = scaled
            dots = dots + jnp.sum(scaled * unit_part, -1, keepdims=True)
        dots = dots / width
        for i in range(tp_count):
            cols = slice(i * slice_width, (i + 1) * slice_width)
            gin_ref[:, cols] = (
                g_ref[me, :, cols].astype(jnp.float32)
                + inverse * (grad_unit[:, cols] - unit[:, cols] * dots)
            ).astype(jnp.bfloat16)

    @pl.when(feeds)
    def _():
        for zd in range(outer):
            next_copy(zd, sec - 1).start()

    @pl.when(fed)
    def _():
        for zd in range(outer):
            next_copy(zd, sec).wait_recv()
            for xd in range(1, inner):
                next_forward(zd, xd).start()
        for zd in range(outer):
            for xd in range(1, inner):
                next_forward(zd, xd).wait()

    @pl.when(feeds)
    def _():
        for zd in range(outer):
            next_copy(zd, sec - 1).wait_send()


def relay(turn, batch_groups, identity, part, dkv, g, saved, gain, kw, vw):
    tp_count, rows, width = part.shape
    tokens = dkv.shape[1]
    slice_width, key_width = kw.shape
    vmem = pl.BlockSpec(memory_space=pltpu.VMEM)
    dma = pltpu.SemaphoreType.DMA((tp_count,))
    outer = tp_count // inner_size(tp_count)
    low = jnp.bfloat16
    return pl.pallas_call(
        functools.partial(relay_kernel, turn, batch_groups, lax.axis_size("section"), tp_count),
        out_shape=[
            jax.ShapeDtypeStruct((rows, width), low),
            jax.ShapeDtypeStruct((tp_count, rows, width), low),
            jax.ShapeDtypeStruct((2, tokens, key_width), low),
            jax.ShapeDtypeStruct((1, width), jnp.float32),
        ],
        in_specs=[vmem] * 7,
        out_specs=[vmem] * 4,
        scratch_shapes=[
            pltpu.VMEM((tp_count, rows, width), low),
            pltpu.VMEM((outer, rows, width), low),
            pltpu.VMEM((outer, rows, width), low),
            pltpu.VMEM((tp_count, 2, tokens, HEAD_WIDTH), low),
            pltpu.VMEM((tp_count, rows, slice_width), low),
            pltpu.VMEM((tp_count, rows, slice_width), low),
            pltpu.VMEM((rows, width), jnp.float32),
            pltpu.VMEM((rows, width), jnp.float32),
        ]
        + [dma] * 12,
        compiler_params=pltpu.CompilerParams(
            collective_id=identity, has_side_effects=True, vmem_limit_bytes=VMEM_LIMIT
        ),
        name=f"relay_{turn}",
    )(*lax.optimization_barrier((part, dkv, g, saved, gain, kw, vw)))


def body(
    section_inputs,
    norm_gain,
    w_query,
    key_projection,
    value_projection,
    w_out,
    token_dir,
    tok_logratio,
    segment_ids,
    pair_of_slot,
    pair_counts,
):
    low, wide = jnp.bfloat16, jnp.float32
    section_count = lax.axis_size("section")
    tp_count = lax.axis_size("tp")
    section_index = lax.axis_index("section")
    tp_index = lax.axis_index("tp")
    saved = section_inputs[0]
    batch_groups, rows, width = saved.shape
    token_total = rows * tp_count
    every = batch_groups * token_total
    gain_values = norm_gain[0].astype(wide)
    query_weight = w_query[0]
    key_weight = key_projection[0]
    value_weight = value_projection[0]
    out_weight = w_out[0]
    head_cols = query_weight.shape[1]
    local_heads = head_cols // HEAD_WIDTH
    slice_width, key_width = key_weight.shape
    key_count = key_width // HEAD_WIDTH
    sharers = tp_count // key_count
    seq_count = 2 * SLOTS
    scale = 1.0 / math.sqrt(HEAD_WIDTH)

    ratio_rows = jnp.broadcast_to(tok_logratio.reshape(-1, 1), (batch_groups * rows, 128))
    saved_all, ratio_all, dir_all = exchange(
        (saved, ratio_rows, token_dir), ("all", "all", "last"), 1, 0
    )
    whole = saved_all.transpose(1, 0, 2, 3).reshape(every, width)
    ratios = (
        ratio_all[:, :, 0]
        .reshape(tp_count, batch_groups, rows)
        .transpose(1, 0, 2)
        .reshape(batch_groups, token_total)
    )
    whole_wide = whole.astype(wide)
    whole_inverse = lax.rsqrt(jnp.mean(whole_wide * whole_wide, -1, keepdims=True) + norm_epsilon)
    normed = (whole_wide * whole_inverse * gain_values).astype(low)
    normed_cols = lax.dynamic_slice_in_dim(normed, tp_index * slice_width, slice_width, 1)
    kv_parts = [
        jnp.dot(normed_cols, weight, preferred_element_type=wide).astype(low)
        for weight in (key_weight, value_weight)
    ]
    keys, values = (
        jnp.sum(every_part.astype(wide), 0)
        .astype(low)
        .reshape(batch_groups, token_total, HEAD_WIDTH)
        for every_part in exchange(kv_parts, ("pick", "pick"), sharers, 1)
    )
    queries = jnp.dot(normed, query_weight, preferred_element_type=wide).astype(low)

    member = (
        segment_ids[:, :, None] == jnp.arange(seq_count, dtype=jnp.int32)[None, None, :]
    ).astype(wide)
    seq_sums = jnp.sum(ratios[:, :, None] * member, 1)
    weights = pair_weights(seq_sums, pair_of_slot, pair_counts)
    token_weight = jnp.sum(member * weights[:, None, :], -1)
    top = (
        token_weight.reshape(batch_groups, tp_count, rows)[:, :, :, None]
        * dir_all.transpose(1, 0, 2, 3).astype(wide)
    ).astype(low)

    query_heads = queries.reshape(batch_groups, token_total, local_heads, HEAD_WIDTH)
    position = jnp.arange(token_total, dtype=jnp.int32)
    allowed = (segment_ids[:, :, None] == segment_ids[:, None, :]) & (
        position[:, None] >= position[None, :]
    )[None]
    scores = jnp.einsum("mthc,muc->mhtu", query_heads, keys, preferred_element_type=wide) * scale
    scores = jnp.where(allowed[:, None], scores, masked_score)
    probs = jnp.exp(scores)
    probs = probs / jnp.sum(probs, -1, keepdims=True)
    probs_low = probs.astype(low)
    attended = (
        jnp.einsum("mhtu,muc->mthc", probs_low, values, preferred_element_type=wide)
        .astype(low)
        .reshape(every, head_cols)
    )
    is_last = section_index == section_count - 1
    gain_row = norm_gain[0].reshape(1, width)

    def select(array, pick):
        return lax.dynamic_index_in_dim(array, pick, 0, keepdims=False)

    boundary = jnp.zeros((tp_count, rows, width), low)
    turns = []
    for turn in range(section_count + batch_groups - 1):
        pick = jnp.clip(turn - (section_count - 1 - section_index), 0, batch_groups - 1)
        incoming = jnp.where(is_last, top[min(turn, batch_groups - 1)], boundary)
        upstream = incoming.reshape(token_total, width)
        grad_heads = (
            contract_last(upstream, out_weight)
            .astype(low)
            .reshape(token_total, local_heads, HEAD_WIDTH)
        )
        query_now = select(query_heads, pick)
        key_now = select(keys, pick)
        value_now = select(values, pick)
        probs_now = select(probs, pick)
        probs_low_now = select(probs_low, pick)
        grad_probs = jnp.einsum("thc,uc->htu", grad_heads, value_now, preferred_element_type=wide)
        grad_scores = probs_now * (
            grad_probs - jnp.sum(probs_now * grad_probs, -1, keepdims=True)
        )
        scores_low = (grad_scores * scale).astype(low)
        grad_query_heads = jnp.einsum(
            "htu,uc->htc", scores_low, key_now, preferred_element_type=wide
        ).astype(low)
        grad_query = grad_query_heads.transpose(1, 0, 2).reshape(token_total, head_cols)
        dkv = jnp.stack(
            [
                jnp.einsum("htu,thc->uc", scores_low, query_now, preferred_element_type=wide),
                jnp.einsum("htu,thc->uc", probs_low_now, grad_heads, preferred_element_type=wide),
            ]
        ).astype(low)
        part = contract_last(grad_query, query_weight).astype(low)
        relayed = relay(
            turn,
            batch_groups,
            2 + turn,
            part.reshape(tp_count, rows, width),
            dkv,
            incoming,
            select(saved, pick),
            gain_row,
            key_weight,
            value_weight,
        )
        grad_rows, boundary, dkv_full, gain_part = lax.optimization_barrier(tuple(relayed))
        turns.append((grad_rows, upstream, dkv_full, gain_part, grad_query_heads))

    begin = section_count - 1 - section_index
    grads, upstreams, dkvs, gains, grad_queries = (
        lax.dynamic_slice_in_dim(jnp.stack(values_of), begin, batch_groups, 0)
        for values_of in zip(*turns)
    )
    gain_total = jnp.sum(gains, 0).reshape(8, width // 8)
    (gain_all,) = exchange((gain_total,), ("all",), 1, 2 + len(turns))
    outer = functools.partial(
        lax.dot_general,
        dimension_numbers=(((0,), (0,)), ((), ())),
        preferred_element_type=wide,
    )
    return (
        grads[None],
        outer(normed, grad_queries.transpose(0, 2, 1, 3).reshape(every, head_cols)).astype(low)[None],
        outer(normed_cols, dkvs[:, 0].reshape(every, key_width)).astype(low)[None],
        outer(normed_cols, dkvs[:, 1].reshape(every, key_width)).astype(low)[None],
        outer(attended, upstreams.reshape(every, width)).astype(low)[None],
        jnp.sum(gain_all, 0).reshape(1, width),
    )


def solution(mesh):
    placed = (
        P("section", None, "tp", None),
        P("section", None),
        P("section", None, "tp"),
        P("section", "tp", None),
        P("section", "tp", None),
        P("section", "tp", None),
        P(None, "tp", None),
        P(None, "tp"),
        P(),
        P(),
        P(),
    )
    return jax.shard_map(
        body,
        mesh=mesh,
        in_specs=placed,
        out_specs=(
            P("section", None, "tp", None),
            P("section", None, "tp"),
            P("section", "tp", None),
            P("section", "tp", None),
            P("section", "tp", None),
            P("section", None),
        ),
        check_vma=False,
    )
```
